768 devices in a mesh: dp: 64 (over y, z_hi, x), seq: 12 (over z_lo, core).
Axes of the slice: x: 4, y: 8, z: 12 (z_hi: 2, z_lo: 6; z = z_hi * 6 + z_lo), core: 2. Of those that a mesh axis runs over, the one named last changes fastest.
Arguments:
- tiles: bfloat16 [64, 24, 64, 588], P('dp', 'seq'), may hold values from -6 to 6
- tile_list: int32 [64, 24], P('dp'), may hold values from 0 to 23, each once within a row
- valid_tiles: int32 [64], P('dp'), may hold values from 2 to 24, as said below
- patch_weight: bfloat16 [768, 588], replicated, may hold values from -0.25 to 0.25
- norm_gain: float32 [768], replicated, may hold values from 0.25 to 1.75
- norm_bias: float32 [768], replicated, may hold values from -3 to 3
- w_query: bfloat16 [768, 768], replicated
- w_key: bfloat16 [768, 768], replicated
- w_value: bfloat16 [768, 768], replicated, may hold values from -0.21875 to 0.21875
- w_out: bfloat16 [768, 768], replicated, may hold values from -0.21875 to 0.21875
- cotangent: bfloat16 [64, 1536, 768], P('dp', 'seq'), may hold values from -16 to 16
Outputs:
- patch_grad: float32 [768, 588], P('dp')
The draws below stay inside these ranges and needn't reach their ends.
Inputs may be any that keep to these rules, and one draw needn't show every extreme that they name: `tile_list`: each row is a permutation of the 24 storage indices. `valid_tiles`: some scene holds data in all 24 tiles and some in only 2.
All inputs are finite; a program needn't handle non-finite values.
Results may differ from the reference program's by a relative error of at most 0.012.
The reference program's roundings to bfloat16 on the way count: a program that leaves them out, or rounds other values in their place, can miss the bound.
Values may be sent and summed in bfloat16 or wider, within the bound.
No kernel may reach another device: no remote copies, remote signals or barrier semaphores. Data moves between devices by JAX's collectives and lax.ppermute only.
A program may use at most 32 MiB of HBM per device.

```python
import jax
import jax.numpy as jnp
from jax import lax

D = 768
HEADS = 12
HEAD_DIM = 64
INNER = 768
PATCH_IN = 588
TILE_TOK = 64
TILES_DEV = 2
TILES = 24
SEQ = 1536
SCENES = 64


def draw_tiles(key, part):
    shape = (SCENES, TILES, TILE_TOK, PATCH_IN)
    base = jax.random.normal(jax.random.fold_in(key, 301), shape, jnp.float32)
    return jnp.clip(base, -6.0, 6.0).astype(jnp.bfloat16)


def draw_valid_tiles(key, part):
    first_key = jax.random.fold_in(key, 101)
    second_key = jax.random.fold_in(key, 102)
    third_key = jax.random.fold_in(key, 103)
    counts = jax.random.randint(first_key, (SCENES,), TILES_DEV, TILES + 1)
    full_scene = jax.random.randint(second_key, (), 0, SCENES)
    low_scene = (full_scene + 1 + jax.random.randint(third_key, (), 0, SCENES - 1)) % SCENES
    places = jnp.arange(SCENES)
    counts = jnp.where(places == full_scene, TILES, counts)
    counts = jnp.where(places == low_scene, TILES_DEV, counts)
    return counts.astype(jnp.int32)


def draw_w_query(key, part):
    own_part = jax.random.normal(jax.random.fold_in(key, 211), (D, INNER), jnp.float32)
    scale_in = float(D) ** (-0.5)
    mixed = own_part
    return (mixed * scale_in).astype(jnp.bfloat16)


def draw_w_key(key, part):
    own_part = jax.random.normal(jax.random.fold_in(key, 223), (D, INNER), jnp.float32)
    scale_in = float(D) ** (-0.5)
    mixed = own_part
    return (mixed * scale_in).astype(jnp.bfloat16)


def with_spikes(result, key, source, target, parts, factor):
    def block_of(dim):
        return (jnp.arange(result.shape[dim]) // (result.shape[dim] // parts)).reshape((-1,) + (1,) * (result.ndim - 1 - dim))

    first = jax.random.permutation(key, parts)[block_of(target)]
    far = (block_of(target) + parts // 2) % parts
    return jnp.where((block_of(source) == first) | (block_of(source) == far), factor * result, result)


def level_of(key, dims, pieces, smallest, high):
    loudness = 1.0
    for position, shards_of in pieces:
        steps = jax.random.uniform(jax.random.fold_in(jax.random.fold_in(key, 6), position), (shards_of,), jnp.float32, smallest / len(pieces), high / len(pieces))
        loudness = loudness * jnp.repeat(jnp.exp(steps), dims[position] // shards_of).reshape((-1,) + (1,) * (len(dims) - 1 - position))
    return loudness


def normal_values(key, shape, width, bound, pieces=(), kind=jnp.bfloat16):
    factor_of = level_of(key, shape, pieces, -0.22, 0.18) if pieces else 1.0
    array = jax.random.normal(key, shape, jnp.float32) * width * factor_of
    return jnp.minimum(jnp.maximum(array, -bound), bound).astype(kind)


def gaussian_with(rng, shape, spread, bound, cuts, heavy, kind=jnp.bfloat16):
    array = spread * jax.random.normal(rng, shape, jnp.float32)
    if cuts:
        array = array * level_of(rng, shape, cuts, -0.22, 0.18)
    return jnp.clip(with_spikes(array, jax.random.fold_in(rng, 3), *heavy), -bound, bound).astype(kind)


def setup_inputs(seed: int = 0) -> dict:
    keys = jax.random.split(jax.random.key(seed), 12)
    return {
        "tiles": draw_tiles(jax.random.fold_in(keys[11], 71), 0),
        "tile_list": jax.vmap(lambda own: jax.random.permutation(own, TILES))(jax.random.split(keys[1], SCENES)).reshape((SCENES, TILES)).astype(jnp.int32),
        "valid_tiles": draw_valid_tiles(jax.random.fold_in(keys[11], 71), 0),
        "patch_weight": normal_values(keys[3], (D, PATCH_IN), PATCH_IN ** -0.5, 0.25),
        "norm_gain": jnp.clip(1.0 + 0.15 * jax.random.normal(keys[4], (D,), jnp.float32), 0.25, 1.75),
        "norm_bias": normal_values(keys[5], (D,), 0.5, 3.0, (), jnp.float32),
        "w_query": draw_w_query(jax.random.fold_in(keys[11], 71), 0),
        "w_key": draw_w_key(jax.random.fold_in(keys[11], 71), 0),
        "w_value": normal_values(keys[8], (D, INNER), D ** -0.5, 0.21875),
        "w_out": normal_values(keys[9], (INNER, D), INNER ** -0.5, 0.21875),
        "cotangent": gaussian_with(keys[10], (SCENES, SEQ, D), 1.0, 16.0, ((0, 64), (1, 12)), (0, 2, 64, 4.0)),
    }


eps_norm = 1e-06

def norm_forward(embedded, norm_gain, norm_bias):
    row_mean = lax.optimization_barrier(jnp.mean(embedded, axis=-1, keepdims=True))
    centred = embedded - row_mean
    inv_std = lax.rsqrt(lax.optimization_barrier(jnp.mean(centred * centred, axis=-1, keepdims=True)) + eps_norm)
    normed = centred * inv_std
    return (normed, inv_std, (normed * norm_gain + norm_bias).astype(jnp.bfloat16))

def norm_backward(d_out, normed, inv_std, norm_gain):
    d_normed = d_out * norm_gain
    first_mean = lax.optimization_barrier(jnp.mean(d_normed, axis=-1, keepdims=True))
    second_mean = lax.optimization_barrier(jnp.mean(d_normed * normed, axis=-1, keepdims=True))
    return inv_std * (d_normed - first_mean - normed * second_mean)

def softmax_rows(scores):
    peak = lax.optimization_barrier(jnp.max(scores, axis=-1, keepdims=True))
    expo = jnp.exp(scores - peak)
    return expo / lax.optimization_barrier(jnp.sum(expo, axis=-1, keepdims=True))

def reference(tiles, tile_list, valid_tiles, patch_weight, norm_gain, norm_bias, w_query, w_key, w_value, w_out, cotangent):
    scale_grad = float(SCENES * SEQ) ** (-0.5)
    inv_root = float(HEAD_DIM) ** (-0.5)

    def one_scene(running, inputs):
        scene_tiles, scene_list, scene_valid, scene_cot = inputs
        patches = jnp.take(scene_tiles, scene_list, axis=0).reshape(SEQ, PATCH_IN)
        embedded = jnp.dot(patches, patch_weight.T, preferred_element_type=jnp.float32)
        normed, inv_std, ln_out = norm_forward(embedded, norm_gain, norm_bias)
        queries = jnp.dot(ln_out, w_query, preferred_element_type=jnp.float32).astype(jnp.bfloat16)
        key_rows = jnp.dot(ln_out, w_key, preferred_element_type=jnp.float32).astype(jnp.bfloat16)
        value_rows = jnp.dot(ln_out, w_value, preferred_element_type=jnp.float32).astype(jnp.bfloat16)
        live_rows = jnp.arange(SEQ) < scene_valid * TILE_TOK
        cot_live = jnp.where(live_rows[:, None], scene_cot, jnp.zeros_like(scene_cot))
        d_attn = jnp.dot(cot_live, w_out.T, preferred_element_type=jnp.float32).astype(jnp.bfloat16)
        head_q = queries.reshape(SEQ, HEADS, HEAD_DIM).astype(jnp.float32)
        head_k = key_rows.reshape(SEQ, HEADS, HEAD_DIM).astype(jnp.float32)
        head_v = value_rows.reshape(SEQ, HEADS, HEAD_DIM).astype(jnp.float32)
        head_a = d_attn.reshape(SEQ, HEADS, HEAD_DIM).astype(jnp.float32)
        scores = jnp.einsum('qhd,khd->hqk', head_q, head_k) * inv_root
        scores = jnp.where(live_rows[None, None, :], scores, jnp.float32(-1e+30))
        probs = softmax_rows(scores)
        probs_low = probs.astype(jnp.bfloat16)
        d_probs = jnp.einsum('qhd,khd->hqk', head_a, head_v)
        row_dot = lax.optimization_barrier(jnp.sum(probs * d_probs, axis=-1, keepdims=True))
        d_scores = (probs * (d_probs - row_dot) * inv_root).astype(jnp.bfloat16).astype(jnp.float32)
        d_query = jnp.einsum('hqk,khd->qhd', d_scores, head_k).astype(jnp.bfloat16).reshape(SEQ, INNER)
        d_key = jnp.einsum('hqk,qhd->khd', d_scores, head_q).astype(jnp.bfloat16).reshape(SEQ, INNER)
        d_value = jnp.einsum('hqk,qhd->khd', probs_low.astype(jnp.float32), head_a).astype(jnp.bfloat16).reshape(SEQ, INNER)
        d_ln = jnp.dot(d_query, w_query.T, preferred_element_type=jnp.float32)
        d_ln = d_ln + jnp.dot(d_key, w_key.T, preferred_element_type=jnp.float32)
        d_ln = d_ln + jnp.dot(d_value, w_value.T, preferred_element_type=jnp.float32)
        d_embedded = (cot_live.astype(jnp.float32) + norm_backward(d_ln, normed, inv_std, norm_gain)).astype(jnp.bfloat16)
        term = jnp.dot(d_embedded.T, patches, preferred_element_type=jnp.float32)
        return (running + term, None)
    running, unused = lax.scan(one_scene, jnp.zeros((D, PATCH_IN), jnp.float32), (tiles, tile_list, valid_tiles, cotangent))
    return running * scale_grad
```

```python
import jax
import jax.numpy as jnp
from jax import lax
from jax.experimental import pallas as pl
from jax.experimental.pallas import tpu as pltpu
from jax.sharding import Mesh
from jax.sharding import PartitionSpec as P

HEADS = 12
HEAD_DIM = 64
D = 768
PIX = 588
PIX_PAD = 640
TILES = 24
TILE_TOK = 64
SEQ = TILES * TILE_TOK
EPS = 1e-06
QB = 256
TOK_DEV = 128

DP_AXES = ("y", "zh", "x")
SEQ_AXES = ("zl", "core")


def dot(a, b, ca, cb):
    return lax.dot_general(
        a, b, (((ca,), (cb,)), ((), ())), preferred_element_type=jnp.float32
    )


def scene_kernel(
    list_ref, meta_ref, patch_ref, weight_ref, gain_ref, bias_ref, wqkv_ref, a_ref, cot_ref,
    out_ref,
    p_ref, normed_ref, istd_ref, q_ref, k_ref, v_ref, kt_ref, dqkv_ref, dk_ref, dv_ref, dt_ref,
):
    limit = meta_ref[0]
    position = meta_ref[1]

    def embed_block(c, carry):
        base = pl.multiple_of(c * QB, QB)
        for t in range(QB // TILE_TOK):
            tile = list_ref[c * (QB // TILE_TOK) + t]
            p_ref[pl.ds(base + t * TILE_TOK, TILE_TOK), :] = patch_ref[tile]
        embedded = dot(p_ref[pl.ds(base, QB), :], weight_ref[...], 1, 1)
        mean = jnp.sum(embedded, axis=1, keepdims=True) * (1.0 / D)
        centred = embedded - mean
        var = jnp.sum(centred * centred, axis=1, keepdims=True) * (1.0 / D)
        inv_std = lax.rsqrt(var + EPS)
        normed = centred * inv_std
        ln_out = (normed * gain_ref[...] + bias_ref[...]).astype(jnp.bfloat16)
        normed_ref[pl.ds(base, QB), :] = normed
        istd_ref[pl.ds(base, QB), :] = jnp.broadcast_to(inv_std, (QB, 128))
        qkv = dot(ln_out, wqkv_ref[...], 1, 0)
        q_ref[pl.ds(base, QB), :] = qkv[:, :HEAD_DIM].astype(jnp.bfloat16)
        k_ref[pl.ds(base, QB), :] = qkv[:, HEAD_DIM : 2 * HEAD_DIM].astype(jnp.bfloat16)
        v_ref[pl.ds(base, QB), :] = qkv[:, 2 * HEAD_DIM :].astype(jnp.bfloat16)
        return carry

    lax.fori_loop(0, SEQ // QB, embed_block, 0)
    kt_ref[...] = jnp.transpose(k_ref[...])
    dk_ref[...] = jnp.zeros_like(dk_ref)
    dv_ref[...] = jnp.zeros_like(dv_ref)
    inv_root = HEAD_DIM ** (-0.5)

    def attend_block(c, carry):
        base = pl.multiple_of(c * QB, QB)
        q_block = q_ref[pl.ds(base, QB), :]
        a_block = a_ref[pl.ds(base, QB), :]
        scores = dot(k_ref[...], q_block, 1, 1) * inv_root
        key_row = lax.broadcasted_iota(jnp.int32, (SEQ, QB), 0)
        scores = jnp.where(key_row < limit, scores, -1e30)
        peak = jnp.max(scores, axis=0, keepdims=True)
        expo = jnp.exp(scores - peak)
        probs = expo * (1.0 / jnp.sum(expo, axis=0, keepdims=True))
        d_probs = dot(v_ref[...], a_block, 1, 1)
        row_dot = jnp.sum(probs * d_probs, axis=0, keepdims=True)
        d_scores = (probs * (d_probs - row_dot) * inv_root).astype(jnp.bfloat16)
        dv_ref[...] += dot(probs.astype(jnp.bfloat16), a_block, 1, 0)
        dk_ref[...] += dot(d_scores, q_block, 1, 0)
        d_query = dot(kt_ref[...], d_scores, 1, 0)
        dqkv_ref[pl.ds(base, QB), :HEAD_DIM] = jnp.transpose(d_query).astype(jnp.bfloat16)
        return carry

    lax.fori_loop(0, SEQ // QB, attend_block, 0)
    dqkv_ref[:, HEAD_DIM : 2 * HEAD_DIM] = dk_ref[...].astype(jnp.bfloat16)
    dqkv_ref[:, 2 * HEAD_DIM :] = dv_ref[...].astype(jnp.bfloat16)

    def norm_block(c, carry):
        base = pl.multiple_of(c * TOK_DEV, TOK_DEV)
        d_ln = dot(dqkv_ref[pl.ds(base, TOK_DEV), :], wqkv_ref[...], 1, 1)
        g = d_ln * gain_ref[...]
        normed = normed_ref[pl.ds(base, TOK_DEV), :]
        first = jnp.sum(g, axis=1, keepdims=True) * (1.0 / D)
        second = jnp.sum(g * normed, axis=1, keepdims=True) * (1.0 / D)
        d_emb = istd_ref[pl.ds(base, TOK_DEV), :1] * (g - first - normed * second)
        own = jnp.where(c == position, 1.0, 0.0)
        d_emb = d_emb + cot_ref[...].astype(jnp.float32) * own
        dt_ref[:, pl.ds(base, TOK_DEV)] = jnp.transpose(d_emb).astype(jnp.bfloat16)
        return carry

    lax.fori_loop(0, SEQ // TOK_DEV, norm_block, 0)

    def grad_block(b, carry):
        rows = pl.multiple_of(b * 96, 96)
        part = dot(dt_ref[pl.ds(rows, 96), :], p_ref[...], 1, 0).astype(jnp.bfloat16)
        half = pl.multiple_of(b * 48, 48)
        out_ref[0, pl.ds(half, 48), :] = part[:48]
        out_ref[1, pl.ds(half, 48), :] = part[48:]
        return carry

    lax.fori_loop(0, D // 96, grad_block, 0)


def scene_call(order, meta, patches, weight, gain, bias, wqkv, head_a, cot_live):
    bf, f32 = jnp.bfloat16, jnp.float32
    smem = pl.BlockSpec(memory_space=pltpu.SMEM)
    vmem = pl.BlockSpec(memory_space=pltpu.VMEM)
    return pl.pallas_call(
        scene_kernel,
        out_shape=jax.ShapeDtypeStruct((2, D // 2, PIX_PAD), bf),
        in_specs=[smem, smem] + [vmem] * 7,
        out_specs=vmem,
        scratch_shapes=[
            pltpu.VMEM((SEQ, PIX_PAD), bf),
            pltpu.VMEM((SEQ, D), f32),
            pltpu.VMEM((SEQ, 128), f32),
            pltpu.VMEM((SEQ, HEAD_DIM), bf),
            pltpu.VMEM((SEQ, HEAD_DIM), bf),
            pltpu.VMEM((SEQ, HEAD_DIM), bf),
            pltpu.VMEM((HEAD_DIM, SEQ), bf),
            pltpu.VMEM((SEQ, 3 * HEAD_DIM), bf),
            pltpu.VMEM((SEQ, HEAD_DIM), f32),
            pltpu.VMEM((SEQ, HEAD_DIM), f32),
            pltpu.VMEM((D, SEQ), bf),
        ],
        compiler_params=pltpu.CompilerParams(vmem_limit_bytes=48 << 20),
    )(order, meta, patches, weight, gain, bias, wqkv, head_a, cot_live)


def exchange(x, axes):
    return lax.all_to_all(x, axes, 0, 0, tiled=True)


def gather(x, axes, count):
    copies = jnp.broadcast_to(x[None], (count,) + x.shape)
    return lax.all_to_all(copies, axes, 0, 0, tiled=False)


def per_device(
    tiles, tile_list, valid_tiles, patch_weight, norm_gain, norm_bias,
    w_query, w_key, w_value, w_out, cotangent,
):
    bf, f32 = jnp.bfloat16, jnp.float32
    position = lax.axis_index(SEQ_AXES)
    limit = valid_tiles[0] * TILE_TOK
    pixels = jnp.pad(tiles.reshape(TOK_DEV, PIX), ((0, 0), (0, PIX_PAD - PIX)))
    by_chip = gather(pixels, "zl", 6)
    patches = gather(by_chip.reshape(6 * TOK_DEV, PIX_PAD), "core", 2)
    patches = patches.reshape(2, 6, 2, TILE_TOK, PIX_PAD)

    live_rows = position * TOK_DEV + jnp.arange(TOK_DEV) < limit
    cot_rows = cotangent[0]
    cot_live = jnp.where(live_rows[:, None], cot_rows, jnp.zeros_like(cot_rows))
    d_attn = dot(cot_live, w_out, 1, 1).astype(bf)
    by_head = jnp.transpose(d_attn.reshape(TOK_DEV, HEADS, HEAD_DIM), (1, 0, 2))
    head_a = exchange(by_head, SEQ_AXES).reshape(SEQ, HEAD_DIM)

    start = position * HEAD_DIM
    wqkv = jnp.concatenate(
        [lax.dynamic_slice_in_dim(w, start, HEAD_DIM, 1) for w in (w_query, w_key, w_value)], axis=1
    )
    weight = jnp.pad(patch_weight, ((0, 0), (0, PIX_PAD - PIX)))
    stored = tile_list[0]
    chip = stored // 4
    place = (stored // 2) % 2 * 12 + chip * 2 + stored % 2
    meta = jnp.stack([limit, position])
    patches = patches.reshape(TILES, TILE_TOK, PIX_PAD)
    halves = scene_call(
        place, meta, patches, weight, norm_gain[None], norm_bias[None], wqkv, head_a, cot_live
    )

    pair = exchange(halves, "core")
    mine = (pair[0].astype(f32) + pair[1].astype(f32)).astype(bf)
    along_y = exchange(mine.reshape(8, 48, PIX_PAD), "y")
    row_sum = jnp.sum(along_y.astype(f32), axis=0).astype(bf)
    along_x = exchange(row_sum.reshape(4, 12, PIX_PAD), "x")
    column = jnp.sum(along_x.astype(f32), axis=0).astype(bf)
    along_z = gather(column, ("zh", "zl"), 12)
    total = jnp.sum(along_z.astype(f32), axis=0)
    other = lax.ppermute(total, "core", [(0, 1), (1, 0)])
    same = lax.axis_index("core") == lax.axis_index("zh")
    result = jnp.where(same, total, other)[:, :PIX]
    return result * (float(64 * SEQ) ** (-0.5))


def solution(mesh):
    fine = Mesh(mesh.devices.reshape(8, 2, 4, 6, 2), ("y", "zh", "x", "zl", "core"))
    in_specs = (
        P(DP_AXES, SEQ_AXES, None, None), P(DP_AXES, None), P(DP_AXES),
        P(), P(), P(), P(), P(), P(), P(), P(DP_AXES, SEQ_AXES, None),
    )
    return jax.shard_map(
        per_device, mesh=fine, in_specs=in_specs, out_specs=P(DP_AXES, None), check_vma=False
    )
```

```python
import jax
import jax.numpy as jnp
from jax import lax
from jax.experimental import pallas as pl
from jax.experimental.pallas import tpu as pltpu
from jax.sharding import Mesh
from jax.sharding import PartitionSpec as P

HEADS = 12
HEAD_DIM = 64
D = 768
PIX = 588
PIX_ROW = 592
PIX_PAD = 640
TILES = 24
TILE_TOK = 64
SEQ = TILES * TILE_TOK
HALF = SEQ // 2
EPS = 1e-06
QB = 256
TOK_DEV = 128
EMBED_VMEM = 12 << 20
SCENE_VMEM = 38 << 20

DP_AXES = ("y", "zh", "x")
CHIP_AXES = ("zt", "zi")
SEQ_AXES = ("zt", "zi", "core")


def dot(a, b, ca, cb):
    return lax.dot_general(
        a, b, (((ca,), (cb,)), ((), ())), preferred_element_type=jnp.float32
    )


WQKV = slice(TOK_DEV, TOK_DEV + 3 * HEAD_DIM)
FEATURES = [slice(r * 128, (r + 1) * 128) for r in range(D // 128)]
KEYS = [slice(r * 128, (r + 1) * 128) for r in range(SEQ // 128)]


def wide(x):
    return jnp.concatenate([x, x], axis=1)


def join_blocks(own_ref, other_ref, pixel_ref):
    for b in range(6):
        block = own_ref[b] if b < 3 else other_ref[b - 3]
        pixel_ref[:PIX_ROW, b * 128 : (b + 1) * 128] = block
    pixel_ref[PIX_ROW:, :] = jnp.zeros((PIX_PAD - PIX_ROW, HALF), jnp.bfloat16)


def fold(x):
    return jnp.sum(x.reshape(x.shape[0] // 8, 8, x.shape[1]), axis=0)


def normalise(emb_ref, ln_ref, affine_ref):
    total = sum(fold(emb_ref[rows, :]) for rows in FEATURES)
    mean = jnp.sum(total, axis=0, keepdims=True) * (1.0 / D)
    squares = jnp.zeros((8, QB), jnp.float32)
    for rows in FEATURES:
        centred = emb_ref[rows, :] - mean
        squares = squares + fold(centred * centred)
    var = jnp.sum(squares, axis=0, keepdims=True) * (1.0 / D)
    inv_std = lax.rsqrt(var + EPS)
    for rows in FEATURES:
        normed = (emb_ref[rows, :] - mean) * inv_std
        emb_ref[rows, :] = normed
        ln_out = normed * wide(affine_ref[0, rows, :]) + wide(affine_ref[1, rows, :])
        ln_ref[rows, :] = ln_out.astype(jnp.bfloat16)
    return mean, inv_std


def start_loads(sources, targets, sems):
    copies = [
        pltpu.make_async_copy(source, target, sems.at[i])
        for i, (source, target) in enumerate(zip(sources, targets, strict=True))
    ]
    for copy in copies:
        copy.start()
    return copies


def embed_kernel(
    own_hbm, other_hbm, weight_hbm, pack_hbm, affine_hbm,
    mean_ref, istd_ref, qkv_ref, pixel_ref, emb_ref, ln_ref,
    own_ref, other_ref, weight_ref, pack_ref, affine_ref, sems, wqkv_t_ref,
):
    loads = start_loads(
        (own_hbm, other_hbm, weight_hbm, pack_hbm, affine_hbm),
        (own_ref, other_ref, weight_ref, pack_ref, affine_ref),
        sems,
    )
    for load in loads:
        load.wait()
    wqkv_t_ref[...] = jnp.transpose(pack_ref[:, WQKV])
    join_blocks(own_ref, other_ref, pixel_ref)
    chunks = [slice(c * QB, (c + 1) * QB) for c in range(HALF // QB)]
    for c, at in enumerate(chunks):
        emb_ref[c] = dot(weight_ref[...], pixel_ref[:, at], 1, 0)
    for c, at in enumerate(chunks):
        mean, inv_std = normalise(emb_ref.at[c], ln_ref.at[c], affine_ref)
        mean_ref[:, at] = mean
        istd_ref[:, at] = inv_std
        qkv_ref[:, at] = dot(wqkv_t_ref[...], ln_ref[c], 1, 0).astype(jnp.bfloat16)


def embed_call(own, other, weight, affine, packed):
    bf, f32 = jnp.bfloat16, jnp.float32
    vmem = pl.BlockSpec(memory_space=pltpu.VMEM)
    return pl.pallas_call(
        embed_kernel,
        out_shape=(
            jax.ShapeDtypeStruct((1, HALF), f32),
            jax.ShapeDtypeStruct((1, HALF), f32),
            jax.ShapeDtypeStruct((3 * HEAD_DIM, HALF), bf),
        ),
        in_specs=[pl.BlockSpec(memory_space=pl.ANY)] * 5,
        out_specs=(vmem,) * 3,
        scratch_shapes=[
            pltpu.VMEM((PIX_PAD, HALF), bf),
            pltpu.VMEM((HALF // QB, D, QB), f32),
            pltpu.VMEM((HALF // QB, D, QB), bf),
            *(pltpu.VMEM(x.shape, x.dtype) for x in (own, other, weight, packed, affine)),
            pltpu.SemaphoreType.DMA((5,)),
            pltpu.VMEM((3 * HEAD_DIM, D), bf),
        ],
        compiler_params=pltpu.CompilerParams(vmem_limit_bytes=EMBED_VMEM),
    )(own, other, weight, packed, affine)


def scene_kernel(
    place_ref, meta_ref, mean_a, istd_a, qkv_a,
    far_own_hbm, far_other_hbm, weight_hbm, pack_hbm, affine_hbm,
    near_own_hbm, near_other_hbm, head_hbm,
    keep_ref, send_ref,
    far_own, far_other, weight_ref, pack_ref, affine_ref,
    near_own, near_other, head_ref, sems, wqkv_t_ref,
    pix_a, pix_b, emb_ref, istd_b, qkv_b,
    k_ref, v_ref, kt_ref, qt_ref, q_ref, a_ref, live_ref, dqkv_ref, dk_ref, dv_ref, dt_ref,
    pick_ref, grad_ref, s_ref, dp_ref, p_ref, ds_ref, ln_ref, g_ref,
):
    bf, f32 = jnp.bfloat16, jnp.float32
    valid, position, core = meta_ref[0], meta_ref[1], meta_ref[2]
    inv_root = HEAD_DIM ** (-0.5)
    half_chunks = [slice(c * QB, (c + 1) * QB) for c in range(HALF // QB)]
    chunks = [slice(c * QB, (c + 1) * QB) for c in range(SEQ // QB)]
    steps = len(chunks)

    loads = start_loads(
        (far_own_hbm, far_other_hbm, weight_hbm, pack_hbm, affine_hbm,
         near_own_hbm, near_other_hbm, head_hbm),
        (far_own, far_other, weight_ref, pack_ref, affine_ref,
         near_own, near_other, head_ref),
        sems,
    )
    for load in loads[:3]:
        load.wait()
    join_blocks(far_own, far_other, pix_b)
    for c, at in enumerate(half_chunks):
        emb_ref[c] = dot(weight_ref[...], pix_b[:, at], 1, 0)
    for load in loads[3:]:
        load.wait()
    wqkv_t_ref[...] = jnp.transpose(pack_ref[:, WQKV])
    join_blocks(near_own, near_other, pix_a)
    for b in range(HEADS):
        rows = jnp.transpose(head_ref[b])
        for i in range(2):
            j = 2 * b + i
            base = pl.multiple_of(place_ref[j] * TILE_TOK, TILE_TOK)
            a_ref[pl.ds(base, TILE_TOK), :] = rows[i * TILE_TOK : (i + 1) * TILE_TOK]
            live_ref[pl.ds(base, TILE_TOK), :] = jnp.full(
                (TILE_TOK, 128), jnp.where(j < valid, 1.0, 0.0), f32
            )
    for c, at in enumerate(half_chunks):
        mean, inv_std = normalise(emb_ref.at[c], ln_ref.at[c], affine_ref)
        istd_b[:, at] = inv_std
        qkv_b[:, at] = dot(wqkv_t_ref[...], ln_ref[c], 1, 0).astype(bf)

    for i, qkv in enumerate((qkv_a, qkv_b)):
        at = slice(i * HALF, (i + 1) * HALF)
        qt_ref[:, at] = qkv[:HEAD_DIM, :] * jnp.asarray(inv_root, bf)
        kt_ref[:, at] = qkv[HEAD_DIM : 2 * HEAD_DIM, :]
        kv = jnp.transpose(qkv[HEAD_DIM:, :])
        k_ref[at, :] = kv[:, :HEAD_DIM]
        v_ref[at, :] = kv[:, HEAD_DIM:]
    q_ref[...] = jnp.transpose(qt_ref[...])

    def scores_of(c):
        s_ref[c % 2] = dot(k_ref[...], qt_ref[:, chunks[c]], 1, 0)
        dp_ref[c % 2] = dot(v_ref[...], a_ref[chunks[c], :], 1, 1)

    def softmax_of(c):
        scores, d_probs = s_ref.at[c % 2], dp_ref.at[c % 2]
        peak = jnp.full((8, QB), -1e30, f32)
        for rows in KEYS:
            masked = jnp.where(wide(live_ref[rows, :]) > 0.5, scores[rows, :], -1e30)
            peak = jnp.maximum(peak, jnp.max(masked.reshape(16, 8, QB), axis=0))
        peak = jnp.max(peak, axis=0, keepdims=True)
        total = jnp.zeros((8, QB), f32)
        weighted = jnp.zeros((8, QB), f32)
        for rows in KEYS:
            masked = jnp.where(wide(live_ref[rows, :]) > 0.5, scores[rows, :], -1e30)
            expo = jnp.exp(masked - peak)
            scores[rows, :] = expo
            total = total + fold(expo)
            weighted = weighted + fold(expo * d_probs[rows, :])
        scale = 1.0 / jnp.sum(total, axis=0, keepdims=True)
        row_dot = jnp.sum(weighted, axis=0, keepdims=True) * scale
        for rows in KEYS:
            probs = scores[rows, :] * scale
            p_ref[c % 2, rows, :] = probs.astype(bf)
            ds_ref[c % 2, rows, :] = (probs * (d_probs[rows, :] - row_dot)).astype(bf)

    def grads_of(c):
        d_value = dot(p_ref[c % 2], a_ref[chunks[c], :], 1, 0)
        d_key = dot(ds_ref[c % 2], q_ref[chunks[c], :], 1, 0)
        dv_ref[...] = d_value if c == 0 else dv_ref[...] + d_value
        dk_ref[...] = d_key if c == 0 else dk_ref[...] + d_key
        d_query = dot(kt_ref[...], ds_ref[c % 2], 1, 0) * inv_root
        dqkv_ref[:HEAD_DIM, chunks[c]] = d_query.astype(bf)

    scores_of(0)
    for c in range(steps):
        if c + 1 < steps:
            scores_of(c + 1)
        if c > 0:
            grads_of(c - 1)
        softmax_of(c)
    grads_of(steps - 1)
    dqkv_ref[HEAD_DIM : 2 * HEAD_DIM, :] = jnp.transpose(dk_ref[...]).astype(bf)
    dqkv_ref[2 * HEAD_DIM :, :] = jnp.transpose(dv_ref[...]).astype(bf)

    def norm_grad(c, normed_ref, inv_std):
        slot = c % 2
        g_ref[slot] = dot(pack_ref[:, WQKV], dqkv_ref[:, chunks[c]], 1, 0)
        first = jnp.zeros((8, QB), f32)
        second = jnp.zeros((8, QB), f32)
        for rows in FEATURES:
            g = g_ref[slot, rows, :] * wide(affine_ref[0, rows, :])
            g_ref[slot, rows, :] = g
            first = first + fold(g)
            second = second + fold(g * normed_ref[rows, :])
        first = jnp.sum(first, axis=0, keepdims=True) * (1.0 / D)
        second = jnp.sum(second, axis=0, keepdims=True) * (1.0 / D)
        for rows in FEATURES:
            d_emb = inv_std * (g_ref[slot, rows, :] - first - normed_ref[rows, :] * second)
            dt_ref[rows, chunks[c]] = d_emb.astype(bf)

    for c, at in enumerate(half_chunks):
        norm_grad(c + steps // 2, emb_ref.at[c], istd_b[:, at])
    for c, at in enumerate(half_chunks):
        emb_ref[c] = dot(weight_ref[...], pix_a[:, at], 1, 0)
    grad_ref[...] = dot(dt_ref[:, HALF:], pix_b[...], 1, 1)
    for c, at in enumerate(half_chunks):
        mean, inv_std = mean_a[:, at], istd_a[:, at]
        for rows in FEATURES:
            emb_ref[c, rows, :] = (emb_ref[c, rows, :] - mean) * inv_std
        norm_grad(c, emb_ref.at[c], inv_std)

    lane = lax.broadcasted_iota(jnp.int32, (PIX_PAD, 128), 1)
    for i in range(2):
        spot = place_ref[2 * position + i]
        block = lax.div(spot, 2)
        base = pl.multiple_of(lax.rem(block, 6) * 128, 128)

        def fill(source):
            picked = source[:, pl.ds(base, 128)].astype(f32)
            turned = pltpu.roll(picked, TILE_TOK, 1)
            picked = jnp.where(lax.rem(spot, 2) == i, picked, turned)
            own = (lane < TILE_TOK) if i == 0 else (lane >= TILE_TOK)
            pick_ref[...] = jnp.where(own, picked, pick_ref[...])

        @pl.when(block < 6)
        def _():
            fill(pix_a)

        @pl.when(block >= 6)
        def _():
            fill(pix_b)

    grad_ref[...] += dot(dt_ref[:, :HALF], pix_a[...], 1, 1) + dot(
        pack_ref[:, :TOK_DEV], pick_ref[...].astype(bf), 1, 1
    )
    first_core = core == 0
    for y in range(8):
        for zh in range(2):
            for x in range(4):
                row, spot = 96 * y + 48 * zh + 12 * x, 12 * y + 6 * zh
                low, high = grad_ref[row : row + 6, :], grad_ref[row + 6 : row + 12, :]
                keep_ref[x, spot : spot + 6, :] = jnp.where(first_core, low, high)
                send_ref[x, spot : spot + 6, :] = jnp.where(first_core, high, low).astype(bf)


def scene_call(place, meta, near, far, front, head_t, weight, packed, affine):
    bf, f32 = jnp.bfloat16, jnp.float32
    smem = pl.BlockSpec(memory_space=pltpu.SMEM)
    vmem = pl.BlockSpec(memory_space=pltpu.VMEM)
    loaded = (*far, weight, packed, affine, *near, head_t)
    return pl.pallas_call(
        scene_kernel,
        out_shape=(
            jax.ShapeDtypeStruct((4, 96, PIX_PAD), f32),
            jax.ShapeDtypeStruct((4, 96, PIX_PAD), bf),
        ),
        in_specs=[smem, smem] + [vmem] * 3 + [pl.BlockSpec(memory_space=pl.ANY)] * 8,
        out_specs=(vmem, vmem),
        scratch_shapes=[
            *(pltpu.VMEM(x.shape, x.dtype) for x in loaded),
            pltpu.SemaphoreType.DMA((8,)),
            pltpu.VMEM((3 * HEAD_DIM, D), bf),
            pltpu.VMEM((PIX_PAD, HALF), bf),
            pltpu.VMEM((PIX_PAD, HALF), bf),
            pltpu.VMEM((HALF // QB, D, QB), f32),
            pltpu.VMEM((1, HALF), f32),
            pltpu.VMEM((3 * HEAD_DIM, HALF), bf),
            pltpu.VMEM((SEQ, HEAD_DIM), bf),
            pltpu.VMEM((SEQ, HEAD_DIM), bf),
            pltpu.VMEM((HEAD_DIM, SEQ), bf),
            pltpu.VMEM((HEAD_DIM, SEQ), bf),
            pltpu.VMEM((SEQ, HEAD_DIM), bf),
            pltpu.VMEM((SEQ, HEAD_DIM), bf),
            pltpu.VMEM((SEQ, 128), f32),
            pltpu.VMEM((3 * HEAD_DIM, SEQ), bf),
            pltpu.VMEM((SEQ, HEAD_DIM), f32),
            pltpu.VMEM((SEQ, HEAD_DIM), f32),
            pltpu.VMEM((D, SEQ), bf),
            pltpu.VMEM((PIX_PAD, 128), f32),
            pltpu.VMEM((D, PIX_PAD), f32),
            pltpu.VMEM((2, SEQ, QB), f32),
            pltpu.VMEM((2, SEQ, QB), f32),
            pltpu.VMEM((2, SEQ, QB), bf),
            pltpu.VMEM((2, SEQ, QB), bf),
            pltpu.VMEM((HALF // QB, D, QB), bf),
            pltpu.VMEM((2, D, QB), f32),
        ],
        compiler_params=pltpu.CompilerParams(vmem_limit_bytes=SCENE_VMEM),
    )(place, meta, *front, *loaded)


def exchange(x, axes):
    return lax.all_to_all(x, axes, 0, 0, tiled=True)


def shift_chips(x):
    return [lax.ppermute(x, "zi", [(i, (i + hop) % 3) for i in range(3)]) for hop in (1, 2)]


def swap_core(x):
    return lax.ppermute(x, "core", [(0, 1), (1, 0)])


def place_of(stored, zt, zi, core):
    owner, part = stored // 2, stored % 2
    chip, owner_core = owner // 2, owner % 2
    owner_t, owner_i = chip // 3, chip % 3
    inner = (zi - owner_i + 3) % 3
    block = jnp.where(owner_t == zt, 0, 6) + jnp.where(owner_core == core, 0, 3) + inner
    return (block * 2 + part).astype(jnp.int32)


def sum_over_z(column):
    parts = column.astype(jnp.bfloat16).reshape(2, 1, 6, PIX_PAD)
    parts = jnp.broadcast_to(parts, (2, 6, 6, PIX_PAD)).reshape(12, 6, PIX_PAD)
    own = jnp.sum(exchange(parts, ("zh", "zt", "zi")).astype(jnp.float32), axis=0)
    other = swap_core(own)
    first_core = lax.axis_index("core") == 0
    return jnp.concatenate(
        [jnp.where(first_core, own, other), jnp.where(first_core, other, own)], axis=0
    )


def per_device(
    tiles, tile_list, valid_tiles, patch_weight, norm_gain, norm_bias,
    w_query, w_key, w_value, w_out, cotangent,
):
    bf, f32 = jnp.bfloat16, jnp.float32
    position = lax.axis_index(SEQ_AXES)
    core = lax.axis_index("core")
    zt = lax.axis_index("zt")
    limit = valid_tiles[0] * TILE_TOK

    pixels = jnp.pad(tiles.reshape(TOK_DEV, PIX).T, ((0, PIX_ROW - PIX), (0, 0)))
    across = lax.ppermute(pixels, "zt", [(0, 1), (1, 0)])

    live_rows = position * TOK_DEV + jnp.arange(TOK_DEV) < limit
    cot_rows = cotangent[0]
    cot_live = jnp.where(live_rows[:, None], cot_rows, jnp.zeros_like(cot_rows))
    d_attn_t = dot(w_out, cot_live, 1, 1).astype(bf).reshape(HEADS, HEAD_DIM, TOK_DEV)
    start = position * HEAD_DIM
    parts = [lax.dynamic_slice_in_dim(w, start, HEAD_DIM, 1) for w in (w_query, w_key, w_value)]
    packed = jnp.concatenate([cot_live.T, *parts, jnp.zeros((D, HEAD_DIM), bf)], axis=1)
    weight = jnp.pad(patch_weight, ((0, 0), (0, PIX_PAD - PIX)))
    affine = jnp.broadcast_to(jnp.stack([norm_gain, norm_bias])[:, :, None], (2, D, 128))
    place = place_of(tile_list[0], zt, lax.axis_index("zi"), core)
    meta = jnp.stack([valid_tiles[0], position, core])

    near_own = jnp.stack([pixels, *shift_chips(pixels)])
    head_t = exchange(d_attn_t, SEQ_AXES)
    across, head_t, near_own, packed, weight, affine, place, meta = lax.optimization_barrier(
        (across, head_t, near_own, packed, weight, affine, place, meta)
    )
    shifted = shift_chips(across)
    near = (near_own, swap_core(near_own))
    front = embed_call(*near, weight, affine, packed)
    shifted, front = lax.optimization_barrier((shifted, front))
    far_own = jnp.stack([across, *shifted])
    far = (far_own, swap_core(far_own))
    keep, send = scene_call(
        place, meta, near, far, front, head_t, weight, packed, affine
    )

    got = swap_core(send)
    mine = (keep + got.astype(f32)).astype(bf)
    along_x = exchange(mine, "x")
    row_sum = jnp.sum(along_x.astype(f32), axis=0).astype(bf)
    along_y = exchange(row_sum.reshape(8, 12, PIX_PAD), "y")
    column = jnp.sum(along_y.astype(f32), axis=0)
    total = sum_over_z(column)[:, :PIX]
    return total * (float(64 * SEQ) ** (-0.5))


def solution(mesh):
    fine = Mesh(
        mesh.devices.reshape(8, 2, 4, 2, 3, 2), ("y", "zh", "x", "zt", "zi", "core")
    )
    in_specs = (
        P(DP_AXES, SEQ_AXES, None, None), P(DP_AXES, None), P(DP_AXES),
        P(), P(), P(), P(), P(), P(), P(), P(DP_AXES, SEQ_AXES, None),
    )
    return jax.shard_map(
        per_device, mesh=fine, in_specs=in_specs, out_specs=P(DP_AXES, None), check_vma=False
    )
```

```python
import jax
import jax.numpy as jnp
from jax import lax
from jax.experimental import pallas as pl
from jax.experimental.pallas import tpu as pltpu
from jax.sharding import Mesh
from jax.sharding import PartitionSpec as P

HEADS = 12
HEAD_DIM = 64
D = 768
PIX = 588
PIX_ROW = 592
PIX_PAD = 640
TILES = 24
TILE_TOK = 64
SEQ = TILES * TILE_TOK
HALF = SEQ // 2
EPS = 1e-06
QB = 256
TOK_DEV = 128
EMBED_VMEM = 12 << 20
SCENE_VMEM = 38 << 20

DP_AXES = ("y", "zh", "x")
SEQ_AXES = ("zt", "zi", "core")


def dot(a, b, ca, cb):
    return lax.dot_general(
        a, b, (((ca,), (cb,)), ((), ())), preferred_element_type=jnp.float32
    )


WQKV = slice(TOK_DEV, TOK_DEV + 3 * HEAD_DIM)
FEATURES = [slice(r * 128, (r + 1) * 128) for r in range(D // 128)]
KEYS = [slice(r * 128, (r + 1) * 128) for r in range(SEQ // 128)]


def wide(x):
    return jnp.concatenate([x, x], axis=1)


def join_blocks(own_ref, other_ref, pixel_ref):
    for b in range(6):
        block = own_ref[b] if b < 3 else other_ref[b - 3]
        pixel_ref[:PIX_ROW, b * 128 : (b + 1) * 128] = block
    pixel_ref[PIX_ROW:, :] = jnp.zeros((PIX_PAD - PIX_ROW, HALF), jnp.bfloat16)


def fold(x):
    return jnp.sum(x.reshape(x.shape[0] // 8, 8, x.shape[1]), axis=0)


def normalise(emb_ref, ln_ref, affine_ref):
    total = sum(fold(emb_ref[rows, :]) for rows in FEATURES)
    mean = jnp.sum(total, axis=0, keepdims=True) * (1.0 / D)
    squares = jnp.zeros((8, QB), jnp.float32)
    for rows in FEATURES:
        centred = emb_ref[rows, :] - mean
        squares = squares + fold(centred * centred)
    var = jnp.sum(squares, axis=0, keepdims=True) * (1.0 / D)
    inv_std = lax.rsqrt(var + EPS)
    for rows in FEATURES:
        normed = (emb_ref[rows, :] - mean) * inv_std
        emb_ref[rows, :] = normed
        ln_out = normed * wide(affine_ref[0, rows, :]) + wide(affine_ref[1, rows, :])
        ln_ref[rows, :] = ln_out.astype(jnp.bfloat16)
    return mean, inv_std


def start_loads(sources, targets, sems):
    copies = [
        pltpu.make_async_copy(source, target, sems.at[i])
        for i, (source, target) in enumerate(zip(sources, targets, strict=True))
    ]
    for copy in copies:
        copy.start()
    return copies


def embed_kernel(
    own_hbm, other_hbm, weight_hbm, pack_hbm, affine_hbm,
    mean_ref, istd_ref, qkv_ref, pixel_ref, emb_ref, ln_ref,
    own_ref, other_ref, weight_ref, pack_ref, affine_ref, sems, wqkv_t_ref,
):
    loads = start_loads(
        (own_hbm, other_hbm, weight_hbm, pack_hbm, affine_hbm),
        (own_ref, other_ref, weight_ref, pack_ref, affine_ref),
        sems,
    )
    for load in loads:
        load.wait()
    wqkv_t_ref[...] = jnp.transpose(pack_ref[:, WQKV])
    join_blocks(own_ref, other_ref, pixel_ref)
    chunks = [slice(c * QB, (c + 1) * QB) for c in range(HALF // QB)]
    for c, at in enumerate(chunks):
        emb_ref[c] = dot(weight_ref[...], pixel_ref[:, at], 1, 0)
    for c, at in enumerate(chunks):
        mean, inv_std = normalise(emb_ref.at[c], ln_ref.at[c], affine_ref)
        mean_ref[:, at] = mean
        istd_ref[:, at] = inv_std
        qkv_ref[:, at] = dot(wqkv_t_ref[...], ln_ref[c], 1, 0).astype(jnp.bfloat16)


def embed_call(own, other, weight, affine, packed):
    bf, f32 = jnp.bfloat16, jnp.float32
    vmem = pl.BlockSpec(memory_space=pltpu.VMEM)
    return pl.pallas_call(
        embed_kernel,
        out_shape=(
            jax.ShapeDtypeStruct((1, HALF), f32),
            jax.ShapeDtypeStruct((1, HALF), f32),
            jax.ShapeDtypeStruct((3 * HEAD_DIM, HALF), bf),
        ),
        in_specs=[pl.BlockSpec(memory_space=pl.ANY)] * 5,
        out_specs=(vmem,) * 3,
        scratch_shapes=[
            pltpu.VMEM((PIX_PAD, HALF), bf),
            pltpu.VMEM((HALF // QB, D, QB), f32),
            pltpu.VMEM((HALF // QB, D, QB), bf),
            *(pltpu.VMEM(x.shape, x.dtype) for x in (own, other, weight, packed, affine)),
            pltpu.SemaphoreType.DMA((5,)),
            pltpu.VMEM((3 * HEAD_DIM, D), bf),
        ],
        compiler_params=pltpu.CompilerParams(vmem_limit_bytes=EMBED_VMEM),
    )(own, other, weight, packed, affine)


def scene_kernel(
    place_ref, meta_ref, mean_a, istd_a, qkv_a,
    far_own_hbm, far_other_hbm, weight_hbm, pack_hbm, affine_hbm,
    near_own_hbm, near_other_hbm, head_hbm,
    keep_ref, send_ref,
    far_own, far_other, weight_ref, pack_ref, affine_ref,
    near_own, near_other, head_ref, sems, wqkv_t_ref,
    pix_a, pix_b, emb_ref, istd_b, qkv_b,
    k_ref, v_ref, kt_ref, qt_ref, q_ref, a_ref, live_ref, dqkv_ref, dk_ref, dv_ref, dt_ref,
    pick_ref, grad_ref, s_ref, dp_ref, p_ref, ds_ref, ln_ref, g_ref,
):
    bf, f32 = jnp.bfloat16, jnp.float32
    valid, position, core = meta_ref[0], meta_ref[1], meta_ref[2]
    inv_root = HEAD_DIM ** (-0.5)
    half_chunks = [slice(c * QB, (c + 1) * QB) for c in range(HALF // QB)]
    chunks = [slice(c * QB, (c + 1) * QB) for c in range(SEQ // QB)]
    steps = len(chunks)

    loads = start_loads(
        (far_own_hbm, far_other_hbm, weight_hbm, pack_hbm, affine_hbm,
         near_own_hbm, near_other_hbm, head_hbm),
        (far_own, far_other, weight_ref, pack_ref, affine_ref,
         near_own, near_other, head_ref),
        sems,
    )
    for load in loads[:3]:
        load.wait()
    join_blocks(far_own, far_other, pix_b)
    for c, at in enumerate(half_chunks):
        emb_ref[c] = dot(weight_ref[...], pix_b[:, at], 1, 0)
    for load in loads[3:]:
        load.wait()
    wqkv_t_ref[...] = jnp.transpose(pack_ref[:, WQKV])
    join_blocks(near_own, near_other, pix_a)
    for b in range(HEADS):
        rows = jnp.transpose(head_ref[b])
        for i in range(2):
            j = 2 * b + i
            base = pl.multiple_of(place_ref[j] * TILE_TOK, TILE_TOK)
            a_ref[pl.ds(base, TILE_TOK), :] = rows[i * TILE_TOK : (i + 1) * TILE_TOK]
            live_ref[pl.ds(base, TILE_TOK), :] = jnp.full(
                (TILE_TOK, 128), jnp.where(j < valid, 1.0, 0.0), f32
            )
    for c, at in enumerate(half_chunks):
        mean, inv_std = normalise(emb_ref.at[c], ln_ref.at[c], affine_ref)
        istd_b[:, at] = inv_std
        qkv_b[:, at] = dot(wqkv_t_ref[...], ln_ref[c], 1, 0).astype(bf)

    for i, qkv in enumerate((qkv_a, qkv_b)):
        at = slice(i * HALF, (i + 1) * HALF)
        qt_ref[:, at] = qkv[:HEAD_DIM, :] * jnp.asarray(inv_root, bf)
        kt_ref[:, at] = qkv[HEAD_DIM : 2 * HEAD_DIM, :]
        kv = jnp.transpose(qkv[HEAD_DIM:, :])
        k_ref[at, :] = kv[:, :HEAD_DIM]
        v_ref[at, :] = kv[:, HEAD_DIM:]
    q_ref[...] = jnp.transpose(qt_ref[...])

    def scores_of(c):
        s_ref[c % 2] = dot(k_ref[...], qt_ref[:, chunks[c]], 1, 0)
        dp_ref[c % 2] = dot(v_ref[...], a_ref[chunks[c], :], 1, 1)

    def softmax_of(c):
        scores, d_probs = s_ref.at[c % 2], dp_ref.at[c % 2]
        peak = jnp.full((8, QB), -1e30, f32)
        for rows in KEYS:
            masked = jnp.where(wide(live_ref[rows, :]) > 0.5, scores[rows, :], -1e30)
            peak = jnp.maximum(peak, jnp.max(masked.reshape(16, 8, QB), axis=0))
        peak = jnp.max(peak, axis=0, keepdims=True)
        total = jnp.zeros((8, QB), f32)
        weighted = jnp.zeros((8, QB), f32)
        for rows in KEYS:
            masked = jnp.where(wide(live_ref[rows, :]) > 0.5, scores[rows, :], -1e30)
            expo = jnp.exp(masked - peak)
            scores[rows, :] = expo
            total = total + fold(expo)
            weighted = weighted + fold(expo * d_probs[rows, :])
        scale = 1.0 / jnp.sum(total, axis=0, keepdims=True)
        row_dot = jnp.sum(weighted, axis=0, keepdims=True) * scale
        for rows in KEYS:
            probs = scores[rows, :] * scale
            p_ref[c % 2, rows, :] = probs.astype(bf)
            ds_ref[c % 2, rows, :] = (probs * (d_probs[rows, :] - row_dot)).astype(bf)

    def grads_of(c):
        d_value = dot(p_ref[c % 2], a_ref[chunks[c], :], 1, 0)
        d_key = dot(ds_ref[c % 2], q_ref[chunks[c], :], 1, 0)
        dv_ref[...] = d_value if c == 0 else dv_ref[...] + d_value
        dk_ref[...] = d_key if c == 0 else dk_ref[...] + d_key
        d_query = dot(kt_ref[...], ds_ref[c % 2], 1, 0) * inv_root
        dqkv_ref[:HEAD_DIM, chunks[c]] = d_query.astype(bf)

    scores_of(0)
    for c in range(steps):
        if c + 1 < steps:
            scores_of(c + 1)
        if c > 0:
            grads_of(c - 1)
        softmax_of(c)
    grads_of(steps - 1)
    dqkv_ref[HEAD_DIM : 2 * HEAD_DIM, :] = jnp.transpose(dk_ref[...]).astype(bf)
    dqkv_ref[2 * HEAD_DIM :, :] = jnp.transpose(dv_ref[...]).astype(bf)

    def norm_grad(c, normed_ref, inv_std):
        slot = c % 2
        g_ref[slot] = dot(pack_ref[:, WQKV], dqkv_ref[:, chunks[c]], 1, 0)
        first = jnp.zeros((8, QB), f32)
        second = jnp.zeros((8, QB), f32)
        for rows in FEATURES:
            g = g_ref[slot, rows, :] * wide(affine_ref[0, rows, :])
            g_ref[slot, rows, :] = g
            first = first + fold(g)
            second = second + fold(g * normed_ref[rows, :])
        first = jnp.sum(first, axis=0, keepdims=True) * (1.0 / D)
        second = jnp.sum(second, axis=0, keepdims=True) * (1.0 / D)
        for rows in FEATURES:
            d_emb = inv_std * (g_ref[slot, rows, :] - first - normed_ref[rows, :] * second)
            dt_ref[rows, chunks[c]] = d_emb.astype(bf)

    for c, at in enumerate(half_chunks):
        norm_grad(c + steps // 2, emb_ref.at[c], istd_b[:, at])
    for c, at in enumerate(half_chunks):
        emb_ref[c] = dot(weight_ref[...], pix_a[:, at], 1, 0)
    grad_ref[...] = dot(dt_ref[:, HALF:], pix_b[...], 1, 1)
    for c, at in enumerate(half_chunks):
        mean, inv_std = mean_a[:, at], istd_a[:, at]
        for rows in FEATURES:
            emb_ref[c, rows, :] = (emb_ref[c, rows, :] - mean) * inv_std
        norm_grad(c, emb_ref.at[c], inv_std)

    lane = lax.broadcasted_iota(jnp.int32, (PIX_PAD, 128), 1)
    for i in range(2):
        spot = place_ref[2 * position + i]
        block = lax.div(spot, 2)
        base = pl.multiple_of(lax.rem(block, 6) * 128, 128)

        def fill(source):
            picked = source[:, pl.ds(base, 128)].astype(f32)
            turned = pltpu.roll(picked, TILE_TOK, 1)
            picked = jnp.where(lax.rem(spot, 2) == i, picked, turned)
            own = (lane < TILE_TOK) if i == 0 else (lane >= TILE_TOK)
            pick_ref[...] = jnp.where(own, picked, pick_ref[...])

        @pl.when(block < 6)
        def _():
            fill(pix_a)

        @pl.when(block >= 6)
        def _():
            fill(pix_b)

    grad_ref[...] += dot(dt_ref[:, :HALF], pix_a[...], 1, 1) + dot(
        pack_ref[:, :TOK_DEV], pick_ref[...].astype(bf), 1, 1
    )
    first_core = core == 0
    for y in range(8):
        for zh in range(2):
            for x in range(4):
                row, spot = 96 * y + 48 * zh + 12 * x, 12 * y + 6 * zh
                low, high = grad_ref[row : row + 6, :], grad_ref[row + 6 : row + 12, :]
                keep_ref[x, spot : spot + 6, :] = jnp.where(first_core, low, high)
                send_ref[x, spot : spot + 6, :] = jnp.where(first_core, high, low).astype(bf)


def scene_call(place, meta, near, far, front, head_t, weight, packed, affine):
    bf, f32 = jnp.bfloat16, jnp.float32
    smem = pl.BlockSpec(memory_space=pltpu.SMEM)
    vmem = pl.BlockSpec(memory_space=pltpu.VMEM)
    loaded = (*far, weight, packed, affine, *near, head_t)
    return pl.pallas_call(
        scene_kernel,
        out_shape=(
            jax.ShapeDtypeStruct((4, 96, PIX_PAD), f32),
            jax.ShapeDtypeStruct((4, 96, PIX_PAD), bf),
        ),
        in_specs=[smem, smem] + [vmem] * 3 + [pl.BlockSpec(memory_space=pl.ANY)] * 8,
        out_specs=(vmem, vmem),
        scratch_shapes=[
            *(pltpu.VMEM(x.shape, x.dtype) for x in loaded),
            pltpu.SemaphoreType.DMA((8,)),
            pltpu.VMEM((3 * HEAD_DIM, D), bf),
            pltpu.VMEM((PIX_PAD, HALF), bf),
            pltpu.VMEM((PIX_PAD, HALF), bf),
            pltpu.VMEM((HALF // QB, D, QB), f32),
            pltpu.VMEM((1, HALF), f32),
            pltpu.VMEM((3 * HEAD_DIM, HALF), bf),
            pltpu.VMEM((SEQ, HEAD_DIM), bf),
            pltpu.VMEM((SEQ, HEAD_DIM), bf),
            pltpu.VMEM((HEAD_DIM, SEQ), bf),
            pltpu.VMEM((HEAD_DIM, SEQ), bf),
            pltpu.VMEM((SEQ, HEAD_DIM), bf),
            pltpu.VMEM((SEQ, HEAD_DIM), bf),
            pltpu.VMEM((SEQ, 128), f32),
            pltpu.VMEM((3 * HEAD_DIM, SEQ), bf),
            pltpu.VMEM((SEQ, HEAD_DIM), f32),
            pltpu.VMEM((SEQ, HEAD_DIM), f32),
            pltpu.VMEM((D, SEQ), bf),
            pltpu.VMEM((PIX_PAD, 128), f32),
            pltpu.VMEM((D, PIX_PAD), f32),
            pltpu.VMEM((2, SEQ, QB), f32),
            pltpu.VMEM((2, SEQ, QB), f32),
            pltpu.VMEM((2, SEQ, QB), bf),
            pltpu.VMEM((2, SEQ, QB), bf),
            pltpu.VMEM((HALF // QB, D, QB), bf),
            pltpu.VMEM((2, D, QB), f32),
        ],
        compiler_params=pltpu.CompilerParams(vmem_limit_bytes=SCENE_VMEM),
    )(place, meta, *front, *loaded)


def exchange(x, axes):
    return lax.all_to_all(x, axes, 0, 0, tiled=True)


def shift_chips(x):
    return [lax.ppermute(x, "zi", [(i, (i + hop) % 3) for i in range(3)]) for hop in (1, 2)]


def swap_core(x):
    return lax.ppermute(x, "core", [(0, 1), (1, 0)])


def place_of(stored, zt, zi, core):
    owner, part = stored // 2, stored % 2
    chip, owner_core = owner // 2, owner % 2
    owner_t, owner_i = chip // 3, chip % 3
    inner = (zi - owner_i + 3) % 3
    block = jnp.where(owner_t == zt, 0, 6) + jnp.where(owner_core == core, 0, 3) + inner
    return (block * 2 + part).astype(jnp.int32)


def sum_over_z(column):
    parts = column.astype(jnp.bfloat16).reshape(2, 1, 6, PIX_PAD)
    parts = jnp.broadcast_to(parts, (2, 6, 6, PIX_PAD)).reshape(12, 6, PIX_PAD)
    own = jnp.sum(exchange(parts, ("zh", "zt", "zi")).astype(jnp.float32), axis=0)
    other = swap_core(own)
    first_core = lax.axis_index("core") == 0
    return jnp.concatenate(
        [jnp.where(first_core, own, other), jnp.where(first_core, other, own)], axis=0
    )


def per_device(
    tiles, tile_list, valid_tiles, patch_weight, norm_gain, norm_bias,
    w_query, w_key, w_value, w_out, cotangent,
):
    bf, f32 = jnp.bfloat16, jnp.float32
    position = lax.axis_index(SEQ_AXES)
    core = lax.axis_index("core")
    zt = lax.axis_index("zt")
    limit = valid_tiles[0] * TILE_TOK

    pixels = jnp.pad(tiles.reshape(TOK_DEV, PIX).T, ((0, PIX_ROW - PIX), (0, 0)))
    across = lax.ppermute(pixels, "zt", [(0, 1), (1, 0)])
    near_shifts = shift_chips(pixels)

    live_rows = position * TOK_DEV + jnp.arange(TOK_DEV) < limit
    cot_rows = cotangent[0]
    cot_live = jnp.where(live_rows[:, None], cot_rows, jnp.zeros_like(cot_rows))
    d_attn_t = dot(w_out, cot_live, 1, 1).astype(bf).reshape(HEADS, HEAD_DIM, TOK_DEV)
    start = position * HEAD_DIM
    parts = [lax.dynamic_slice_in_dim(w, start, HEAD_DIM, 1) for w in (w_query, w_key, w_value)]
    packed = jnp.concatenate([cot_live.T, *parts, jnp.zeros((D, HEAD_DIM), bf)], axis=1)
    weight = jnp.pad(patch_weight, ((0, 0), (0, PIX_PAD - PIX)))
    affine = jnp.broadcast_to(jnp.stack([norm_gain, norm_bias])[:, :, None], (2, D, 128))
    place = place_of(tile_list[0], zt, lax.axis_index("zi"), core)
    meta = jnp.stack([valid_tiles[0], position, core])

    head_t = exchange(d_attn_t, SEQ_AXES)
    near_own = jnp.stack([pixels, *near_shifts])
    across, near_own = lax.optimization_barrier((across, near_own))
    shifted = shift_chips(across)
    near = (near_own, swap_core(near_own))
    packed, weight, affine, near = lax.optimization_barrier((packed, weight, affine, near))
    front = embed_call(*near, weight, affine, packed)
    shifted, front = lax.optimization_barrier((shifted, front))
    far_own = jnp.stack([across, *shifted])
    far = (far_own, swap_core(far_own))
    keep, send = scene_call(
        place, meta, near, far, front, head_t, weight, packed, affine
    )

    got = swap_core(send)
    mine = (keep + got.astype(f32)).astype(bf)
    along_x = exchange(mine, "x")
    row_sum = jnp.sum(along_x.astype(f32), axis=0).astype(bf)
    along_y = exchange(row_sum.reshape(8, 12, PIX_PAD), "y")
    column = jnp.sum(along_y.astype(f32), axis=0)
    total = sum_over_z(column)[:, :PIX]
    return total * (float(64 * SEQ) ** (-0.5))


def solution(mesh):
    fine = Mesh(
        mesh.devices.reshape(8, 2, 4, 2, 3, 2), ("y", "zh", "x", "zt", "zi", "core")
    )
    in_specs = (
        P(DP_AXES, SEQ_AXES, None, None), P(DP_AXES, None), P(DP_AXES),
        P(), P(), P(), P(), P(), P(), P(), P(DP_AXES, SEQ_AXES, None),
    )

    return jax.shard_map(
        per_device, mesh=fine, in_specs=in_specs, out_specs=P(DP_AXES, None), check_vma=False
    )
```

```python
import jax
import jax.numpy as jnp
from jax import lax
from jax.experimental import pallas as pl
from jax.experimental.pallas import tpu as pltpu
from jax.sharding import Mesh
from jax.sharding import PartitionSpec as P

HEADS = 12
HEAD_DIM = 64
D = 768
PIX = 588
PIX_ROW = 592
PIX_PAD = 640
TILES = 24
TILE_TOK = 64
SEQ = TILES * TILE_TOK
HALF = SEQ // 2
EPS = 1e-06
QB = 256
TOK_DEV = 128
EMBED_VMEM = 12 << 20
SCENE_VMEM = 38 << 20

DP_AXES = ("y", "zh", "x")
CHIP_AXES = ("zt", "zi")
SEQ_AXES = ("zt", "zi", "core")


def dot(a, b, ca, cb):
    return lax.dot_general(
        a, b, (((ca,), (cb,)), ((), ())), preferred_element_type=jnp.float32
    )


FEATURES = [slice(r * 128, (r + 1) * 128) for r in range(D // 128)]
KEYS = [slice(r * 128, (r + 1) * 128) for r in range(SEQ // 128)]


def wide(x):
    return jnp.concatenate([x, x], axis=1)


def join_blocks(own_ref, other_ref, pixel_ref):
    for b in range(6):
        block = own_ref[b] if b < 3 else other_ref[b - 3]
        pixel_ref[:PIX_ROW, b * 128 : (b + 1) * 128] = block
    pixel_ref[PIX_ROW:, :] = jnp.zeros((PIX_PAD - PIX_ROW, HALF), jnp.bfloat16)


def fold(x):
    return jnp.sum(x.reshape(x.shape[0] // 8, 8, x.shape[1]), axis=0)


def normalise(emb_ref, ln_ref, affine_ref):
    total = sum(fold(emb_ref[rows, :]) for rows in FEATURES)
    mean = jnp.sum(total, axis=0, keepdims=True) * (1.0 / D)
    squares = jnp.zeros((8, QB), jnp.float32)
    for rows in FEATURES:
        centred = emb_ref[rows, :] - mean
        squares = squares + fold(centred * centred)
    var = jnp.sum(squares, axis=0, keepdims=True) * (1.0 / D)
    inv_std = lax.rsqrt(var + EPS)
    for rows in FEATURES:
        normed = (emb_ref[rows, :] - mean) * inv_std
        emb_ref[rows, :] = normed
        ln_out = normed * wide(affine_ref[0, rows, :]) + wide(affine_ref[1, rows, :])
        ln_ref[rows, :] = ln_out.astype(jnp.bfloat16)
    return mean, inv_std


def start_loads(sources, targets, sems):
    copies = [
        pltpu.make_async_copy(source, target, sems.at[i])
        for i, (source, target) in enumerate(zip(sources, targets, strict=True))
    ]
    for copy in copies:
        copy.start()
    return copies


def unpack_weights(raw_ref, rows_ref, weight_ref, wqkv_ref, wqkv_t_ref, affine_ref):
    weight_ref[...] = jnp.transpose(raw_ref[...])
    for i in range(2):
        affine_ref[i] = jnp.transpose(jnp.broadcast_to(rows_ref[i], (128, D)))
    wqkv_t_ref[...] = jnp.transpose(wqkv_ref[...])


def weight_scratch():
    bf, f32 = jnp.bfloat16, jnp.float32
    return [
        pltpu.VMEM((PIX_PAD, D), bf),
        pltpu.VMEM((2, 1, D), f32),
        pltpu.VMEM((D, PIX_PAD), bf),
        pltpu.VMEM((3 * HEAD_DIM, D), bf),
        pltpu.VMEM((2, D, 128), f32),
    ]


def embed_kernel(
    meta_ref, own_hbm, other_hbm, raw_hbm, gain_hbm, bias_hbm, query_hbm, key_hbm, value_hbm,
    mean_ref, istd_ref, qkv_ref, wqkv_ref,
    raw_ref, rows_ref, weight_ref, wqkv_t_ref, affine_ref,
    three_ref, pixel_ref, emb_ref, ln_ref, own_ref, other_ref, sems,
):
    lanes = pl.ds(pl.multiple_of(meta_ref[3] * 128, 128), 128)
    loads = start_loads(
        (own_hbm, other_hbm, raw_hbm, gain_hbm, bias_hbm,
         query_hbm.at[:, lanes], key_hbm.at[:, lanes], value_hbm.at[:, lanes]),
        (own_ref, other_ref, raw_ref, rows_ref.at[0], rows_ref.at[1],
         three_ref.at[0], three_ref.at[1], three_ref.at[2]),
        sems,
    )
    for load in loads:
        load.wait()
    for i in range(2):

        @pl.when(meta_ref[2] == i)
        def _():
            for j in range(3):
                half = three_ref[j, :, i * HEAD_DIM : (i + 1) * HEAD_DIM]
                wqkv_ref[:, j * HEAD_DIM : (j + 1) * HEAD_DIM] = half

    unpack_weights(raw_ref, rows_ref, weight_ref, wqkv_ref, wqkv_t_ref, affine_ref)
    join_blocks(own_ref, other_ref, pixel_ref)
    chunks = [slice(c * QB, (c + 1) * QB) for c in range(HALF // QB)]
    for c, at in enumerate(chunks):
        emb_ref[c] = dot(weight_ref[...], pixel_ref[:, at], 1, 0)
    for c, at in enumerate(chunks):
        mean, inv_std = normalise(emb_ref.at[c], ln_ref.at[c], affine_ref)
        mean_ref[:, at] = mean
        istd_ref[:, at] = inv_std
        qkv_ref[:, at] = dot(wqkv_t_ref[...], ln_ref[c], 1, 0).astype(jnp.bfloat16)


def embed_call(meta, own, other, params, projections):
    bf, f32 = jnp.bfloat16, jnp.float32
    vmem = pl.BlockSpec(memory_space=pltpu.VMEM)
    return pl.pallas_call(
        embed_kernel,
        out_shape=(
            jax.ShapeDtypeStruct((1, HALF), f32),
            jax.ShapeDtypeStruct((1, HALF), f32),
            jax.ShapeDtypeStruct((3 * HEAD_DIM, HALF), bf),
            jax.ShapeDtypeStruct((D, 3 * HEAD_DIM), bf),
        ),
        in_specs=[pl.BlockSpec(memory_space=pltpu.SMEM)]
        + [pl.BlockSpec(memory_space=pl.ANY)] * 8,
        out_specs=(vmem,) * 4,
        scratch_shapes=[
            *weight_scratch(),
            pltpu.VMEM((3, D, 128), bf),
            pltpu.VMEM((PIX_PAD, HALF), bf),
            pltpu.VMEM((HALF // QB, D, QB), f32),
            pltpu.VMEM((HALF // QB, D, QB), bf),
            pltpu.VMEM(own.shape, bf),
            pltpu.VMEM(other.shape, bf),
            pltpu.SemaphoreType.DMA((8,)),
        ],
        compiler_params=pltpu.CompilerParams(vmem_limit_bytes=EMBED_VMEM),
    )(meta, own, other, *params, *projections)


def scene_kernel(
    place_ref, meta_ref, mean_a, istd_a, qkv_a, wqkv_ref,
    far_own_hbm, far_other_hbm, near_own_hbm, near_other_hbm, head_hbm, cot_hbm,
    raw_hbm, gain_hbm, bias_hbm,
    keep_ref, send_ref,
    far_own, far_other, near_own, near_other, head_ref, cot_ref, sems,
    raw_ref, rows_ref, weight_ref, wqkv_t_ref, affine_ref,
    cot_t_ref,
    pix_a, pix_b, emb_ref, istd_b, qkv_b,
    k_ref, v_ref, kt_ref, qt_ref, q_ref, a_ref, live_ref, dqkv_ref, dk_ref, dv_ref, dt_ref,
    pick_ref, grad_ref, s_ref, dp_ref, p_ref, ds_ref, ln_ref, g_ref,
):
    bf, f32 = jnp.bfloat16, jnp.float32
    valid, position, core = meta_ref[0], meta_ref[1], meta_ref[2]
    inv_root = HEAD_DIM ** (-0.5)
    half_chunks = [slice(c * QB, (c + 1) * QB) for c in range(HALF // QB)]
    chunks = [slice(c * QB, (c + 1) * QB) for c in range(SEQ // QB)]
    steps = len(chunks)

    loads = start_loads(
        (far_own_hbm, far_other_hbm, near_own_hbm, near_other_hbm, head_hbm, cot_hbm,
         raw_hbm, gain_hbm, bias_hbm),
        (far_own, far_other, near_own, near_other, head_ref, cot_ref,
         raw_ref, rows_ref.at[0], rows_ref.at[1]),
        sems,
    )
    for load in loads:
        load.wait()
    unpack_weights(raw_ref, rows_ref, weight_ref, wqkv_ref, wqkv_t_ref, affine_ref)
    token = position * TOK_DEV + lax.broadcasted_iota(jnp.int32, (TOK_DEV, D), 0)
    cot_live = jnp.where(token < valid * TILE_TOK, cot_ref[...].astype(f32), 0.0)
    cot_t_ref[...] = jnp.transpose(cot_live).astype(bf)
    join_blocks(far_own, far_other, pix_b)
    for c, at in enumerate(half_chunks):
        emb_ref[c] = dot(weight_ref[...], pix_b[:, at], 1, 0)
    join_blocks(near_own, near_other, pix_a)
    for b in range(HEADS):
        rows = jnp.transpose(head_ref[b])
        for i in range(2):
            j = 2 * b + i
            base = pl.multiple_of(place_ref[j] * TILE_TOK, TILE_TOK)
            a_ref[pl.ds(base, TILE_TOK), :] = rows[i * TILE_TOK : (i + 1) * TILE_TOK]
            live_ref[pl.ds(base, TILE_TOK), :] = jnp.full(
                (TILE_TOK, 128), jnp.where(j < valid, 1.0, 0.0), f32
            )
    for c, at in enumerate(half_chunks):
        mean, inv_std = normalise(emb_ref.at[c], ln_ref.at[c], affine_ref)
        istd_b[:, at] = inv_std
        qkv_b[:, at] = dot(wqkv_t_ref[...], ln_ref[c], 1, 0).astype(bf)

    for i, qkv in enumerate((qkv_a, qkv_b)):
        at = slice(i * HALF, (i + 1) * HALF)
        qt_ref[:, at] = qkv[:HEAD_DIM, :] * jnp.asarray(inv_root, bf)
        kt_ref[:, at] = qkv[HEAD_DIM : 2 * HEAD_DIM, :]
        kv = jnp.transpose(qkv[HEAD_DIM:, :])
        k_ref[at, :] = kv[:, :HEAD_DIM]
        v_ref[at, :] = kv[:, HEAD_DIM:]
    q_ref[...] = jnp.transpose(qt_ref[...])

    def scores_of(c):
        s_ref[c % 2] = dot(k_ref[...], qt_ref[:, chunks[c]], 1, 0)
        dp_ref[c % 2] = dot(v_ref[...], a_ref[chunks[c], :], 1, 1)

    def softmax_of(c):
        scores, d_probs = s_ref.at[c % 2], dp_ref.at[c % 2]
        peak = jnp.full((8, QB), -1e30, f32)
        for rows in KEYS:
            masked = jnp.where(wide(live_ref[rows, :]) > 0.5, scores[rows, :], -1e30)
            peak = jnp.maximum(peak, jnp.max(masked.reshape(16, 8, QB), axis=0))
        peak = jnp.max(peak, axis=0, keepdims=True)
        total = jnp.zeros((8, QB), f32)
        weighted = jnp.zeros((8, QB), f32)
        for rows in KEYS:
            masked = jnp.where(wide(live_ref[rows, :]) > 0.5, scores[rows, :], -1e30)
            expo = jnp.exp(masked - peak)
            scores[rows, :] = expo
            total = total + fold(expo)
            weighted = weighted + fold(expo * d_probs[rows, :])
        scale = 1.0 / jnp.sum(total, axis=0, keepdims=True)
        row_dot = jnp.sum(weighted, axis=0, keepdims=True) * scale
        for rows in KEYS:
            probs = scores[rows, :] * scale
            p_ref[c % 2, rows, :] = probs.astype(bf)
            ds_ref[c % 2, rows, :] = (probs * (d_probs[rows, :] - row_dot)).astype(bf)

    def grads_of(c):
        d_value = dot(p_ref[c % 2], a_ref[chunks[c], :], 1, 0)
        d_key = dot(ds_ref[c % 2], q_ref[chunks[c], :], 1, 0)
        dv_ref[...] = d_value if c == 0 else dv_ref[...] + d_value
        dk_ref[...] = d_key if c == 0 else dk_ref[...] + d_key
        d_query = dot(kt_ref[...], ds_ref[c % 2], 1, 0) * inv_root
        dqkv_ref[:HEAD_DIM, chunks[c]] = d_query.astype(bf)

    scores_of(0)
    for c in range(steps):
        if c + 1 < steps:
            scores_of(c + 1)
        if c > 0:
            grads_of(c - 1)
        softmax_of(c)
    grads_of(steps - 1)
    dqkv_ref[HEAD_DIM : 2 * HEAD_DIM, :] = jnp.transpose(dk_ref[...]).astype(bf)
    dqkv_ref[2 * HEAD_DIM :, :] = jnp.transpose(dv_ref[...]).astype(bf)

    def norm_grad(c, normed_ref, inv_std):
        slot = c % 2
        g_ref[slot] = dot(wqkv_ref[...], dqkv_ref[:, chunks[c]], 1, 0)
        first = jnp.zeros((8, QB), f32)
        second = jnp.zeros((8, QB), f32)
        for rows in FEATURES:
            g = g_ref[slot, rows, :] * wide(affine_ref[0, rows, :])
            g_ref[slot, rows, :] = g
            first = first + fold(g)
            second = second + fold(g * normed_ref[rows, :])
        first = jnp.sum(first, axis=0, keepdims=True) * (1.0 / D)
        second = jnp.sum(second, axis=0, keepdims=True) * (1.0 / D)
        for rows in FEATURES:
            d_emb = inv_std * (g_ref[slot, rows, :] - first - normed_ref[rows, :] * second)
            dt_ref[rows, chunks[c]] = d_emb.astype(bf)

    for c, at in enumerate(half_chunks):
        norm_grad(c + steps // 2, emb_ref.at[c], istd_b[:, at])
    for c, at in enumerate(half_chunks):
        emb_ref[c] = dot(weight_ref[...], pix_a[:, at], 1, 0)
    grad_ref[...] = dot(dt_ref[:, HALF:], pix_b[...], 1, 1)
    for c, at in enumerate(half_chunks):
        mean, inv_std = mean_a[:, at], istd_a[:, at]
        for rows in FEATURES:
            emb_ref[c, rows, :] = (emb_ref[c, rows, :] - mean) * inv_std
        norm_grad(c, emb_ref.at[c], inv_std)

    lane = lax.broadcasted_iota(jnp.int32, (PIX_PAD, 128), 1)
    for i in range(2):
        spot = place_ref[2 * position + i]
        block = lax.div(spot, 2)
        base = pl.multiple_of(lax.rem(block, 6) * 128, 128)

        def fill(source):
            picked = source[:, pl.ds(base, 128)].astype(f32)
            turned = pltpu.roll(picked, TILE_TOK, 1)
            picked = jnp.where(lax.rem(spot, 2) == i, picked, turned)
            own = (lane < TILE_TOK) if i == 0 else (lane >= TILE_TOK)
            pick_ref[...] = jnp.where(own, picked, pick_ref[...])

        @pl.when(block < 6)
        def _():
            fill(pix_a)

        @pl.when(block >= 6)
        def _():
            fill(pix_b)

    grad_ref[...] += dot(dt_ref[:, :HALF], pix_a[...], 1, 1) + dot(
        cot_t_ref[...], pick_ref[...].astype(bf), 1, 1
    )
    first_core = core == 0
    for y in range(8):
        for zh in range(2):
            for x in range(4):
                row, spot = 96 * y + 48 * zh + 12 * x, 12 * y + 6 * zh
                low, high = grad_ref[row : row + 6, :], grad_ref[row + 6 : row + 12, :]
                keep_ref[x, spot : spot + 6, :] = jnp.where(first_core, low, high)
                send_ref[x, spot : spot + 6, :] = jnp.where(first_core, high, low).astype(bf)


def scene_call(place, meta, near, far, front, head_t, cot, params):
    bf, f32 = jnp.bfloat16, jnp.float32
    smem = pl.BlockSpec(memory_space=pltpu.SMEM)
    vmem = pl.BlockSpec(memory_space=pltpu.VMEM)
    loaded = (*far, *near, head_t, cot)
    return pl.pallas_call(
        scene_kernel,
        out_shape=(
            jax.ShapeDtypeStruct((4, 96, PIX_PAD), f32),
            jax.ShapeDtypeStruct((4, 96, PIX_PAD), bf),
        ),
        in_specs=[smem, smem] + [vmem] * 4 + [pl.BlockSpec(memory_space=pl.ANY)] * 9,
        out_specs=(vmem, vmem),
        scratch_shapes=[
            *(pltpu.VMEM(x.shape, x.dtype) for x in loaded),
            pltpu.SemaphoreType.DMA((9,)),
            *weight_scratch(),
            pltpu.VMEM((D, TOK_DEV), bf),
            pltpu.VMEM((PIX_PAD, HALF), bf),
            pltpu.VMEM((PIX_PAD, HALF), bf),
            pltpu.VMEM((HALF // QB, D, QB), f32),
            pltpu.VMEM((1, HALF), f32),
            pltpu.VMEM((3 * HEAD_DIM, HALF), bf),
            pltpu.VMEM((SEQ, HEAD_DIM), bf),
            pltpu.VMEM((SEQ, HEAD_DIM), bf),
            pltpu.VMEM((HEAD_DIM, SEQ), bf),
            pltpu.VMEM((HEAD_DIM, SEQ), bf),
            pltpu.VMEM((SEQ, HEAD_DIM), bf),
            pltpu.VMEM((SEQ, HEAD_DIM), bf),
            pltpu.VMEM((SEQ, 128), f32),
            pltpu.VMEM((3 * HEAD_DIM, SEQ), bf),
            pltpu.VMEM((SEQ, HEAD_DIM), f32),
            pltpu.VMEM((SEQ, HEAD_DIM), f32),
            pltpu.VMEM((D, SEQ), bf),
            pltpu.VMEM((PIX_PAD, 128), f32),
            pltpu.VMEM((D, PIX_PAD), f32),
            pltpu.VMEM((2, SEQ, QB), f32),
            pltpu.VMEM((2, SEQ, QB), f32),
            pltpu.VMEM((2, SEQ, QB), bf),
            pltpu.VMEM((2, SEQ, QB), bf),
            pltpu.VMEM((HALF // QB, D, QB), bf),
            pltpu.VMEM((2, D, QB), f32),
        ],
        compiler_params=pltpu.CompilerParams(vmem_limit_bytes=SCENE_VMEM),
    )(place, meta, *front, *loaded, *params)


def exchange(x, axes):
    return lax.all_to_all(x, axes, 0, 0, tiled=True)


def shift_chips(x):
    return [lax.ppermute(x, "zi", [(i, (i + hop) % 3) for i in range(3)]) for hop in (1, 2)]


def swap_core(x):
    return lax.ppermute(x, "core", [(0, 1), (1, 0)])


def place_of(stored, zt, zi, core):
    owner, part = stored // 2, stored % 2
    chip, owner_core = owner // 2, owner % 2
    owner_t, owner_i = chip // 3, chip % 3
    inner = (zi - owner_i + 3) % 3
    block = jnp.where(owner_t == zt, 0, 6) + jnp.where(owner_core == core, 0, 3) + inner
    return (block * 2 + part).astype(jnp.int32)


def sum_over_z(column):
    parts = column.astype(jnp.bfloat16).reshape(2, 1, 6, PIX_PAD)
    parts = jnp.broadcast_to(parts, (2, 6, 6, PIX_PAD)).reshape(12, 6, PIX_PAD)
    own = jnp.sum(exchange(parts, ("zh", "zt", "zi")).astype(jnp.float32), axis=0)
    other = swap_core(own)
    first_core = lax.axis_index("core") == 0
    return jnp.concatenate(
        [jnp.where(first_core, own, other), jnp.where(first_core, other, own)], axis=0
    )


def per_device(
    tiles, tile_list, valid_tiles, patch_weight, norm_gain, norm_bias,
    w_query, w_key, w_value, w_out, cotangent,
):
    bf, f32 = jnp.bfloat16, jnp.float32
    position = lax.axis_index(SEQ_AXES)
    core = lax.axis_index("core")
    zt = lax.axis_index("zt")
    limit = valid_tiles[0] * TILE_TOK

    pixels = jnp.pad(tiles.reshape(TOK_DEV, PIX).T, ((0, PIX_ROW - PIX), (0, 0)))
    across = lax.ppermute(pixels, "zt", [(0, 1), (1, 0)])
    near_shifts = shift_chips(pixels)

    live_rows = position * TOK_DEV + jnp.arange(TOK_DEV) < limit
    cot_rows = cotangent[0]
    cot_live = jnp.where(live_rows[:, None], cot_rows, jnp.zeros_like(cot_rows))
    d_attn_t = dot(w_out, cot_live, 1, 1).astype(bf).reshape(HEADS, HEAD_DIM, TOK_DEV)
    head_t = exchange(d_attn_t, SEQ_AXES)
    near_own = jnp.stack([pixels, *near_shifts])
    across, near_own = lax.optimization_barrier((across, near_own))
    shifted = shift_chips(across)
    near = (near_own, swap_core(near_own))

    raw = jnp.pad(patch_weight.T, ((0, PIX_PAD - PIX), (0, 0)))
    params = (raw, norm_gain[None], norm_bias[None])
    place = place_of(tile_list[0], zt, lax.axis_index("zi"), core)
    meta = jnp.stack([valid_tiles[0], position, core, lax.axis_index(CHIP_AXES)])
    front = embed_call(meta, *near, params, (w_query, w_key, w_value))
    shifted, front = lax.optimization_barrier((shifted, front))
    far_own = jnp.stack([across, *shifted])
    far = (far_own, swap_core(far_own))
    keep, send = scene_call(place, meta, near, far, front, head_t, cot_rows, params)

    got = swap_core(send)
    mine = (keep + got.astype(f32)).astype(bf)
    along_x = exchange(mine, "x")
    row_sum = jnp.sum(along_x.astype(f32), axis=0).astype(bf)
    along_y = exchange(row_sum.reshape(8, 12, PIX_PAD), "y")
    column = jnp.sum(along_y.astype(f32), axis=0)
    total = sum_over_z(column)[:, :PIX]
    return total * (float(64 * SEQ) ** (-0.5))


def solution(mesh):
    fine = Mesh(
        mesh.devices.reshape(8, 2, 4, 2, 3, 2), ("y", "zh", "x", "zt", "zi", "core")
    )
    in_specs = (
        P(DP_AXES, SEQ_AXES, None, None), P(DP_AXES, None), P(DP_AXES),
        P(), P(), P(), P(), P(), P(), P(), P(DP_AXES, SEQ_AXES, None),
    )

    return jax.shard_map(
        per_device, mesh=fine, in_specs=in_specs, out_specs=P(DP_AXES, None), check_vma=False
    )
```
